32 devices in a mesh: tm: 8 (over z, x), tensor: 4 (over y, core).
Axes of the slice: x: 2, y: 2, z: 4, core: 2. Of those that a mesh axis runs over, the one named last changes fastest.
Arguments:
- latents: float32 [8, 640, 64], P('tm', 'tensor'), may hold values from -6 to 6
- residual: bfloat16 [8, 640, 5120], P('tm'), may hold values from -6 to 6
- timesteps: int32 [8], P('tm'), may hold values from 0 to 999
- step_sizes: float32 [8], P('tm'), may hold values from 0.015 to 0.06
- embed_weight: bfloat16 [64, 5120], replicated
- mod_weight: bfloat16 [3, 256, 5120], P(None, None, 'tensor'), may hold values from -0.75 to 0.75
- up_weight: bfloat16 [5120, 7168], P('tm', 'tensor'), may hold values from -0.078125 to 0.078125
- down_weight: bfloat16 [7168, 5120], P('tensor', 'tm'), may hold values from -0.0625 to 0.0625
- head_weight: bfloat16 [5120, 64], replicated, may hold values from -0.078125 to 0.078125
Outputs:
- drift: float32 [8, 640, 64], P('tm', 'tensor')
- new_latents: float32 [8, 640, 64], P('tm', 'tensor')
The draws below stay inside these ranges and needn't reach their ends.
All inputs are finite; a program needn't handle non-finite values.
Results may differ from the reference program's by a relative error of at most 0.0085.
Values may be sent and summed in bfloat16 or wider, within the bound.
A program may use at most 128 MiB of HBM per device.

```python
import math
import jax
import jax.numpy as jnp
from jax import lax

D = 5120
FF = 7168
C = 64
FREQ = 256
S = 640
STEPS = 8
N_TENSOR = 4


def draw_embed_weight(key, part):
    first = jax.random.fold_in(key, 11)
    second = jax.random.fold_in(key, 12)
    values = jax.random.normal(first, (C, D), jnp.float32)
    scales = jnp.exp(jax.random.uniform(second, (1, D), jnp.float32, 0.0, math.log(10.0)))
    values = values * scales / 4.0
    return (values / math.sqrt(C)).astype(jnp.bfloat16)


def with_ends(values, rng, low, high):
    spot = [jax.random.randint(jax.random.fold_in(rng, axis), (), 0, length) for axis, length in enumerate(values.shape)]
    widest = values.shape.index(max(values.shape))
    next_to = spot[:widest] + [(spot[widest] + 1) % values.shape[widest]] + spot[widest + 1:]
    return values.at[tuple(spot)].set(low).at[tuple(next_to)].set(high)


def block_levels(rng, extent, pieces, least, high):
    level = 1.0
    for axis_at, shards_of in pieces:
        heights = jax.random.uniform(jax.random.fold_in(jax.random.fold_in(rng, 6), axis_at), (shards_of,), jnp.float32, least / len(pieces), high / len(pieces))
        level = level * jnp.repeat(jnp.exp(heights), extent[axis_at] // shards_of).reshape((-1,) + (1,) * (len(extent) - 1 - axis_at))
    return level


def centred(own_key, dims, deviation, limit, split=(), held_as=jnp.bfloat16):
    array = jax.random.normal(own_key, dims, jnp.float32) * deviation
    if len(split) > 0:
        array = block_levels(own_key, dims, split, -0.22, 0.18) * array
    return jnp.clip(array, min=-limit, max=limit).astype(held_as)


def setup_inputs(seed: int = 0) -> dict:
    key_list = jax.random.split(jax.random.key(seed), 10)
    return {
        "latents": centred(key_list[0], (STEPS, S, C), 1.0, 6.0, ((0, 8), (1, 4)), jnp.float32),
        "residual": centred(key_list[1], (STEPS, S, D), 1.0, 6.0, ((0, 8),)),
        "timesteps": with_ends(jax.random.randint(key_list[2], (STEPS,), 0, 1000), jax.random.fold_in(key_list[2], 1), 0, 999).astype(jnp.int32),
        "step_sizes": jnp.clip(jnp.exp(math.log(0.06) - 1.3862944 * jax.random.uniform(key_list[3], (STEPS,), jnp.float32) ** block_levels(key_list[3], (STEPS,), ((0, 8),), -0.2, 0.2)), 0.015, 0.06),
        "embed_weight": draw_embed_weight(jax.random.fold_in(key_list[9], 71), 0),
        "mod_weight": centred(key_list[5], (3, FREQ, D), (FREQ // 4) ** -0.5, 0.75, ((2, 4),)),
        "up_weight": centred(key_list[6], (D, FF), D ** -0.5, 0.078125, ((0, 8), (1, 4))),
        "down_weight": centred(key_list[7], (FF, D), FF ** -0.5, 0.0625, ((0, 4), (1, 8))),
        "head_weight": centred(key_list[8], (D, C), D ** -0.5, 0.078125),
    }


def normalize(values):
    centre = values - lax.optimization_barrier(jnp.mean(values, axis=-1, keepdims=True))
    spread = lax.optimization_barrier(jnp.mean(centre * centre, axis=-1, keepdims=True))
    return centre * lax.rsqrt(spread + 1e-06)

def time_features(stamps, width):
    half = width // 2
    freqs = jnp.exp(-math.log(10000.0) * jnp.arange(half, dtype=jnp.float32) / half)
    angles = stamps.astype(jnp.float32)[:, None] * freqs[None, :]
    return jnp.concatenate([jnp.cos(angles), jnp.sin(angles)], axis=-1)

def reference(latents, residual, timesteps, step_sizes, embed_weight, mod_weight, up_weight, down_weight, head_weight):
    features = jax.nn.silu(time_features(timesteps, FREQ)).astype(jnp.bfloat16)

    def one_step(items):
        latent, stream, feature = items
        modulation = jnp.einsum('f,kfd->kd', feature.astype(jnp.float32), mod_weight.astype(jnp.float32))
        hidden = stream.astype(jnp.float32) + jnp.dot(latent.astype(jnp.bfloat16), embed_weight, preferred_element_type=jnp.float32)
        normed = (normalize(hidden) * (1.0 + modulation[1]) + modulation[0]).astype(jnp.bfloat16)
        preact = jnp.dot(normed, up_weight, preferred_element_type=jnp.float32)
        activated = jax.nn.gelu(preact, approximate=True).astype(jnp.bfloat16)
        width = FF // N_TENSOR
        mixed = jnp.zeros(hidden.shape, jnp.float32)
        for block in range(N_TENSOR):
            block_sum = jnp.dot(activated[:, block * width:(block + 1) * width], down_weight[block * width:(block + 1) * width], preferred_element_type=jnp.float32)
            rounded = lax.optimization_barrier(block_sum.astype(jnp.bfloat16))
            mixed = mixed + rounded.astype(jnp.float32)
        updated = hidden + modulation[2] * mixed
        return jnp.dot(normalize(updated).astype(jnp.bfloat16), head_weight, preferred_element_type=jnp.float32)
    drift = lax.map(one_step, (latents, residual, features))
    new_latents = latents[0][None] - jnp.cumsum(step_sizes[:, None, None] * drift, axis=0)
    return (drift, new_latents)
```

```python
import math

import jax
import jax.numpy as jnp
from jax import lax
from jax.sharding import PartitionSpec as P


def normalize(values):
    centre = values - jnp.mean(values, axis=-1, keepdims=True)
    spread = jnp.mean(centre * centre, axis=-1, keepdims=True)
    return centre * lax.rsqrt(spread + 1e-06)


def time_features(stamps, width):
    half = width // 2
    freqs = jnp.exp(-math.log(10000.0) * jnp.arange(half, dtype=jnp.float32) / half)
    angles = stamps.astype(jnp.float32)[:, None] * freqs[None, :]
    return jnp.concatenate([jnp.cos(angles), jnp.sin(angles)], axis=-1)


def line_pairs(length, step, rightwards):
    if rightwards:
        return [(z, z + 1) for z in range(step - 1, length - 1)]
    return [(z, z - 1) for z in range(1, length - step + 1)]


def line_gather(block, place, length, after=None):
    def hop(values, pairs):
        both = [(2 * a + x, 2 * b + x) for a, b in pairs for x in range(2)]
        return lax.ppermute(values, "tm", both)

    found = [(place, block)]
    right = left = block
    for step in range(1, length):
        right_pairs = line_pairs(length, step, True)
        left_pairs = line_pairs(length, step, False)
        near = place >= step
        if 2 * step <= length + 1:
            right = hop(right, right_pairs)
            left = hop(left, left_pairs)
            if 2 * step >= length:
                right = left = jnp.where(near, right, left)
        else:
            right = left = hop(right, right_pairs + left_pairs)
        if 2 * step >= length:
            index = jnp.where(near, place - step, place + step)
            found.append((jnp.clip(index, 0, length - 1), right))
        else:
            found.append((jnp.maximum(place - step, 0), right))
            found.append((jnp.minimum(place + step, length - 1), left))
    return found


def slot_of(target, place, length):
    gap = target - place
    far = jnp.abs(gap)
    split = (length - 1) // 2
    apart = jnp.where(gap < 0, 2 * far - 1, 2 * far)
    return jnp.where(gap == 0, 0, jnp.where(far <= split, apart, split + far))


def tensor_sum(part, place, count):
    total = part.astype(jnp.float32)
    size = count
    shift = 1
    while size > 1:
        rows = total.shape[1] // size
        grouped = total.reshape(total.shape[0], size // 2, 2, rows, total.shape[2])
        bit = (place // shift) % 2
        mine = lax.dynamic_index_in_dim(grouped, bit, 2, False)
        theirs = lax.dynamic_index_in_dim(grouped, 1 - bit, 2, False)
        got = lax.ppermute(
            theirs.astype(jnp.bfloat16), "tensor", [(t, t ^ shift) for t in range(count)]
        )
        total = mine + got.astype(jnp.float32)
        total = total.reshape(total.shape[0], (size // 2) * rows, total.shape[3])
        size //= 2
        shift *= 2
    return total


def make_local(n_tm, n_tensor):
    line = n_tm // 2
    swap = [(i, i ^ 1) for i in range(n_tm)]

    def local(
        latents,
        residual,
        timesteps,
        step_sizes,
        embed_weight,
        mod_weight,
        up_weight,
        down_weight,
        head_weight,
    ):
        position = lax.axis_index("tm")
        column = lax.axis_index("tensor")
        place, side = position // 2, position % 2
        latent = latents[0]
        stream = residual[0]
        tokens, width = stream.shape
        own_rows = latent.shape[0]
        depth = up_weight.shape[0]

        ups = line_gather(up_weight, place, line)
        gate_open = ups[-1][1]
        down_first, _ = lax.optimization_barrier((down_weight, gate_open))
        downs = line_gather(down_first, place, line)

        feature = jax.nn.silu(time_features(timesteps, mod_weight.shape[1])).astype(jnp.bfloat16)[0]
        piece_mod = jnp.einsum("f,kfd->kd", feature, mod_weight, preferred_element_type=jnp.float32)
        modulation = lax.all_gather(piece_mod, "tensor", axis=1, tiled=True)
        latent_bf = latent.astype(jnp.bfloat16)
        every_latent = lax.all_gather(latent_bf, "tensor", axis=0, tiled=True)
        every_hidden = stream.astype(jnp.float32) + jnp.dot(
            every_latent, embed_weight, preferred_element_type=jnp.float32
        )
        normed = (normalize(every_hidden) * (1.0 + modulation[1]) + modulation[0]).astype(
            jnp.bfloat16
        )
        row_start = column * own_rows
        hidden = lax.dynamic_slice_in_dim(stream, row_start, own_rows, 0).astype(
            jnp.float32
        ) + jnp.dot(latent_bf, embed_weight, preferred_element_type=jnp.float32)

        halves = normed.reshape(tokens, line, 2, depth).transpose(2, 1, 0, 3)
        mine = lax.dynamic_index_in_dim(halves, side, 0, False)
        theirs = lax.dynamic_index_in_dim(halves, 1 - side, 0, False)
        both = jnp.concatenate([mine, lax.ppermute(theirs, "tm", swap)], axis=1)

        preact = None
        for index, block in ups:
            term = jnp.dot(
                lax.dynamic_index_in_dim(both, index, 0, False),
                block,
                preferred_element_type=jnp.float32,
            )
            preact = term if preact is None else preact + term
        other = lax.ppermute(preact[tokens:].astype(jnp.bfloat16), "tm", swap)
        activated = jax.nn.gelu(
            preact[:tokens] + other.astype(jnp.float32), approximate=True
        ).astype(jnp.bfloat16)
        every_act = jnp.concatenate([activated, lax.ppermute(activated, "tm", swap)], axis=0)

        near, far = [], []
        group = -(-len(downs) // 5)
        for start in range(0, len(downs), group):
            parts = [
                jnp.dot(every_act, block, preferred_element_type=jnp.float32).astype(jnp.bfloat16)
                for _, block in downs[start : start + group]
            ]
            part = jnp.concatenate(parts, axis=-1).reshape(2, tokens, -1)
            summed = tensor_sum(part, column, n_tensor)
            crossed = lax.ppermute(summed[1].astype(jnp.bfloat16), "tm", swap)
            for k in range(len(parts)):
                cut = slice(k * depth, (k + 1) * depth)
                near.append(summed[0][:, cut])
                far.append(crossed[:, cut].astype(jnp.float32))
        near, far = jnp.stack(near), jnp.stack(far)
        pieces = []
        for target in range(line):
            slot = slot_of(target, place, line)
            a = lax.dynamic_index_in_dim(near, slot, 0, False)
            b = lax.dynamic_index_in_dim(far, slot, 0, False)
            pieces.append(jnp.where(side == 0, a, b))
            pieces.append(jnp.where(side == 0, b, a))
        mixed = jnp.concatenate(pieces, axis=-1)

        updated = hidden + modulation[2] * mixed
        drift = jnp.dot(
            normalize(updated).astype(jnp.bfloat16), head_weight, preferred_element_type=jnp.float32
        )
        first = (position == 0).astype(jnp.float32)
        term = first * latent - step_sizes[0] * drift
        gathered = lax.all_gather(term, "tm")
        earlier = (jnp.arange(n_tm) <= position)[:, None, None]
        new_latent = jnp.sum(jnp.where(earlier, gathered, 0.0), axis=0)
        return (drift[None], new_latent[None])

    return local


def solution(mesh):
    in_specs = (
        P("tm", "tensor", None),
        P("tm", None, None),
        P("tm"),
        P("tm"),
        P(),
        P(None, None, "tensor"),
        P("tm", "tensor"),
        P("tensor", "tm"),
        P(),
    )
    out_specs = (P("tm", "tensor", None), P("tm", "tensor", None))
    local = make_local(mesh.shape["tm"], mesh.shape["tensor"])
    return jax.shard_map(local, mesh=mesh, in_specs=in_specs, out_specs=out_specs, check_vma=False)
```

```python
import math

import jax
import jax.numpy as jnp
from jax import lax
from jax.sharding import PartitionSpec as P


def normalize(values):
    centre = values - jnp.mean(values, axis=-1, keepdims=True)
    spread = jnp.mean(centre * centre, axis=-1, keepdims=True)
    return centre * lax.rsqrt(spread + 1e-06)


def time_features(stamps, width):
    half = width // 2
    freqs = jnp.exp(-math.log(10000.0) * jnp.arange(half, dtype=jnp.float32) / half)
    angles = stamps.astype(jnp.float32)[:, None] * freqs[None, :]
    return jnp.concatenate([jnp.cos(angles), jnp.sin(angles)], axis=-1)


def tensor_sum(part, place, count):
    total = part.astype(jnp.float32)
    size = count
    shift = 1
    while size > 1:
        rows = total.shape[1] // size
        grouped = total.reshape(total.shape[0], size // 2, 2, rows, total.shape[2])
        bit = (place // shift) % 2
        mine = lax.dynamic_index_in_dim(grouped, bit, 2, False)
        theirs = lax.dynamic_index_in_dim(grouped, 1 - bit, 2, False)
        got = lax.ppermute(
            theirs.astype(jnp.bfloat16), "tensor", [(t, t ^ shift) for t in range(count)]
        )
        total = mine + got.astype(jnp.float32)
        total = total.reshape(total.shape[0], (size // 2) * rows, total.shape[3])
        size //= 2
        shift *= 2
    return total


def by_slot(blocks, place):
    bit = 1
    while bit < len(blocks):
        take = (place // bit) % 2 == 1
        blocks = [jnp.where(take, blocks[k ^ bit], blocks[k]) for k in range(len(blocks))]
        bit *= 2
    return blocks


def tensor_rows(part, place, count):
    slots, rows, cols = part.shape
    shift = count // 2
    part = part[:, None]
    while shift >= 1:
        got = lax.ppermute(part, "tensor", [(t, t ^ shift) for t in range(count)])
        low = (place // shift) % 2 == 0
        pair = [jnp.where(low, part, got), jnp.where(low, got, part)]
        part = jnp.stack(pair, axis=2).reshape(slots, -1, rows, cols)
        shift //= 2
    return part.reshape(slots, count * rows, cols)


def make_local(n_tm, n_tensor):
    line = n_tm // 2
    swap = [(i, i ^ 1) for i in range(n_tm)]
    pair = [(i, i ^ 2) for i in range(n_tm)]

    def reach(values, k):
        return lax.ppermute(values, "tm", [(i, i ^ (2 * k)) for i in range(n_tm)])

    def local(
        latents,
        residual,
        timesteps,
        step_sizes,
        embed_weight,
        mod_weight,
        up_weight,
        down_weight,
        head_weight,
    ):
        position = lax.axis_index("tm")
        column = lax.axis_index("tensor")
        place, side = position // 2, position % 2
        even = place % 2 == 0
        latent = latents[0]
        stream = residual[0]
        tokens, width = stream.shape
        own_rows = latent.shape[0]
        depth = up_weight.shape[0]
        half = up_weight.shape[1] // 2
        first_cut = -(-half // 256) * 128
        cuts = [(0, first_cut), (first_cut, half)]

        ups = []
        before = None
        for a, b in cuts:
            low, high = up_weight[:, a:b], up_weight[:, half + a : half + b]
            kept, given = jnp.where(even, low, high), jnp.where(even, high, low)
            found = [kept]
            for k in range(1, line):
                block = given if k % 2 else kept
                if before is not None:
                    block, _ = lax.optimization_barrier((block, before[k]))
                found.append(reach(block, k))
            ups.append(found)
            before = found
        parity = place % 2
        kept = lax.dynamic_slice_in_dim(down_weight, parity * half, half, 0)
        given = lax.dynamic_slice_in_dim(down_weight, (1 - parity) * half, half, 0)
        downs = [kept]
        for k in range(1, line):
            block, _ = lax.optimization_barrier((given if k % 2 else kept, before[k]))
            downs.append(reach(block, k))

        feature = jax.nn.silu(time_features(timesteps, mod_weight.shape[1])).astype(jnp.bfloat16)[0]
        piece_mod = jnp.einsum("f,kfd->kd", feature, mod_weight, preferred_element_type=jnp.float32)
        modulation = lax.all_gather(piece_mod, "tensor", axis=1, tiled=True)
        latent_bf = latent.astype(jnp.bfloat16)
        every_latent = lax.all_gather(latent_bf, "tensor", axis=0, tiled=True)

        def modulate(values):
            return (normalize(values) * (1.0 + modulation[1]) + modulation[0]).astype(jnp.bfloat16)

        def halves(values):
            blocks = [values[:, k * depth : (k + 1) * depth] for k in range(2 * line)]
            mine = [jnp.where(side == 0, blocks[2 * k], blocks[2 * k + 1]) for k in range(line)]
            other = [jnp.where(side == 0, blocks[2 * k + 1], blocks[2 * k]) for k in range(line)]
            return by_slot(mine, place), by_slot(other, place)

        row_start = column * own_rows
        hidden = lax.dynamic_slice_in_dim(stream, row_start, own_rows, 0).astype(
            jnp.float32
        ) + jnp.dot(latent_bf, embed_weight, preferred_element_type=jnp.float32)
        mine, other = halves(modulate(hidden))
        from_side = lax.ppermute(jnp.stack(other), "tm", swap)
        from_pair = lax.ppermute(jnp.stack(mine), "tm", pair)
        from_both = lax.ppermute(from_side, "tm", pair)
        every_hidden = stream.astype(jnp.float32) + jnp.dot(
            every_latent, embed_weight, preferred_element_type=jnp.float32
        )
        own, _ = halves(modulate(every_hidden))
        side_rows = tensor_rows(from_side, column, n_tensor)
        pair_rows = tensor_rows(from_pair, column, n_tensor)
        both_rows = tensor_rows(from_both, column, n_tensor)
        groups = [
            [jnp.concatenate([own[k], side_rows[k]], axis=0) for k in range(line)],
            [jnp.concatenate([pair_rows[k ^ 1], both_rows[k ^ 1]], axis=0) for k in range(line)],
        ]

        acts = []
        for rows in groups:
            pieces = []
            for found in ups:
                preact = None
                for k in range(line):
                    term = jnp.dot(rows[k], found[k], preferred_element_type=jnp.float32)
                    preact = term if preact is None else preact + term
                came = lax.ppermute(preact[tokens:].astype(jnp.bfloat16), "tm", swap)
                activated = jax.nn.gelu(
                    preact[:tokens] + came.astype(jnp.float32), approximate=True
                ).astype(jnp.bfloat16)
                across = lax.ppermute(activated, "tm", swap)
                pieces.append(jnp.concatenate([activated, across], axis=0))
            acts.append(jnp.concatenate(pieces, axis=1))

        near, far = [], []
        bunch = max(line // 2, 2)
        for start in range(0, line, bunch):
            slots = range(start, start + bunch)
            sums = []
            for act in acts:
                parts = [
                    jnp.dot(act, downs[k], preferred_element_type=jnp.float32).astype(jnp.bfloat16)
                    for k in slots
                ]
                part = jnp.concatenate(parts, axis=-1).reshape(2, tokens, -1)
                sums.append(tensor_sum(part, column, n_tensor))
            back = lax.ppermute(sums[1].astype(jnp.bfloat16), "tm", pair).astype(jnp.float32)
            count = len(slots)
            back = jnp.concatenate(
                [back[:, :, (j ^ 1) * depth : ((j ^ 1) + 1) * depth] for j in range(count)], axis=-1
            )
            total = sums[0] + back
            crossed = lax.ppermute(total[1].astype(jnp.bfloat16), "tm", swap).astype(jnp.float32)
            for j in range(count):
                near.append(total[0][:, j * depth : (j + 1) * depth])
                far.append(crossed[:, j * depth : (j + 1) * depth])
        near, far = by_slot(near, place), by_slot(far, place)
        pieces = []
        for a, b in zip(near, far):
            pieces.append(jnp.where(side == 0, a, b))
            pieces.append(jnp.where(side == 0, b, a))
        mixed = jnp.concatenate(pieces, axis=-1)

        updated = hidden + modulation[2] * mixed
        drift = jnp.dot(
            normalize(updated).astype(jnp.bfloat16), head_weight, preferred_element_type=jnp.float32
        )
        first = (position == 0).astype(jnp.float32)
        term = first * latent - step_sizes[0] * drift
        beside = lax.ppermute(term, "tm", swap)
        couple = term + beside
        new_latent = term + jnp.where(side == 1, beside, 0.0)
        for k in range(1, line):
            ahead = [(i, i + 2 * k) for i in range(n_tm - 2 * k)]
            new_latent = new_latent + lax.ppermute(couple, "tm", ahead)
        return (drift[None], new_latent[None])

    return local


def solution(mesh):
    in_specs = (
        P("tm", "tensor", None),
        P("tm", None, None),
        P("tm"),
        P("tm"),
        P(),
        P(None, None, "tensor"),
        P("tm", "tensor"),
        P("tensor", "tm"),
        P(),
    )
    out_specs = (P("tm", "tensor", None), P("tm", "tensor", None))
    local = make_local(mesh.shape["tm"], mesh.shape["tensor"])
    return jax.shard_map(local, mesh=mesh, in_specs=in_specs, out_specs=out_specs, check_vma=False)
```

```python
import math

import jax
import jax.numpy as jnp
from jax import lax
from jax.sharding import PartitionSpec as P


def normalize(values):
    centre = values - jnp.mean(values, axis=-1, keepdims=True)
    spread = jnp.mean(centre * centre, axis=-1, keepdims=True)
    return centre * lax.rsqrt(spread + 1e-06)


def time_features(stamps, width):
    half = width // 2
    freqs = jnp.exp(-math.log(10000.0) * jnp.arange(half, dtype=jnp.float32) / half)
    angles = stamps.astype(jnp.float32)[:, None] * freqs[None, :]
    return jnp.concatenate([jnp.cos(angles), jnp.sin(angles)], axis=-1)


def row_order(count):
    order, shift = [0], count // 2
    while shift >= 1:
        order = order + [j ^ shift for j in order]
        shift //= 2
    return order


def tensor_sum(kept, given, count):
    shift = 1
    while shift < count:
        got = lax.ppermute(
            given.astype(jnp.bfloat16), "tensor", [(t, t ^ shift) for t in range(count)]
        )
        kept = kept.astype(jnp.float32) + got.astype(jnp.float32)
        rows = kept.shape[1] // 2
        shift *= 2
        if shift < count:
            kept, given = kept[:, :rows], kept[:, rows:]
    return kept


def by_slot(blocks, place):
    bit = 1
    while bit < len(blocks):
        take = (place // bit) % 2 == 1
        blocks = [jnp.where(take, blocks[k ^ bit], blocks[k]) for k in range(len(blocks))]
        bit *= 2
    return blocks


def tensor_rows(part, count):
    shift = count // 2
    while shift >= 1:
        got = lax.ppermute(part, "tensor", [(t, t ^ shift) for t in range(count)])
        part = jnp.concatenate([part, got], axis=1)
        shift //= 2
    return part


def make_local(n_tm, n_tensor):
    line = n_tm // 2
    swap = [(i, i ^ 1) for i in range(n_tm)]
    pair = [(i, i ^ 2) for i in range(n_tm)]

    def reach(values, k):
        return lax.ppermute(values, "tm", [(i, i ^ (2 * k)) for i in range(n_tm)])

    def local(
        latents,
        residual,
        timesteps,
        step_sizes,
        embed_weight,
        mod_weight,
        up_weight,
        down_weight,
        head_weight,
    ):
        position = lax.axis_index("tm")
        column = lax.axis_index("tensor")
        place, side = position // 2, position % 2
        even = place % 2 == 0
        latent = latents[0]
        stream = residual[0]
        tokens, width = stream.shape
        own_rows = latent.shape[0]
        depth = up_weight.shape[0]
        half = up_weight.shape[1] // 2
        first_cut = -(-half // 256) * 128
        cuts = [(0, first_cut), (first_cut, half)]

        ups = []
        before = None
        for a, b in cuts:
            low, high = up_weight[:, a:b], up_weight[:, half + a : half + b]
            kept, given = jnp.where(even, low, high), jnp.where(even, high, low)
            found = [kept]
            for k in range(1, line):
                block = given if k % 2 else kept
                if before is not None:
                    block, _ = lax.optimization_barrier((block, before[k]))
                found.append(reach(block, k))
            ups.append(found)
            before = found
        parity = place % 2
        kept = lax.dynamic_slice_in_dim(down_weight, parity * half, half, 0)
        given = lax.dynamic_slice_in_dim(down_weight, (1 - parity) * half, half, 0)
        downs = [kept]
        for k in range(1, line):
            block, _ = lax.optimization_barrier((given if k % 2 else kept, before[k]))
            downs.append(reach(block, k))

        feature = jax.nn.silu(time_features(timesteps, mod_weight.shape[1])).astype(jnp.bfloat16)[0]
        piece_mod = jnp.einsum("f,kfd->kd", feature, mod_weight, preferred_element_type=jnp.float32)
        modulation = lax.all_gather(piece_mod, "tensor", axis=1, tiled=True)
        latent_bf = latent.astype(jnp.bfloat16)
        every_latent = lax.all_gather(latent_bf, "tensor", axis=0, tiled=True)

        def modulate(values):
            return (normalize(values) * (1.0 + modulation[1]) + modulation[0]).astype(jnp.bfloat16)

        def halves(values):
            blocks = [values[:, k * depth : (k + 1) * depth] for k in range(2 * line)]
            mine = [jnp.where(side == 0, blocks[2 * k], blocks[2 * k + 1]) for k in range(line)]
            other = [jnp.where(side == 0, blocks[2 * k + 1], blocks[2 * k]) for k in range(line)]
            return by_slot(mine, place), by_slot(other, place)

        row_start = column * own_rows
        hidden = lax.dynamic_slice_in_dim(stream, row_start, own_rows, 0).astype(
            jnp.float32
        ) + jnp.dot(latent_bf, embed_weight, preferred_element_type=jnp.float32)
        mine, other = halves(modulate(hidden))
        from_side = lax.ppermute(jnp.stack(other), "tm", swap)
        from_pair = lax.ppermute(jnp.stack(mine), "tm", pair)
        from_both = lax.ppermute(from_side, "tm", pair)
        order = row_order(n_tensor)

        def reorder(values):
            blocks = [values[t * own_rows : (t + 1) * own_rows] for t in range(n_tensor)]
            blocks = by_slot(blocks, column)
            return jnp.concatenate([blocks[j] for j in order], axis=0)

        every_hidden = reorder(stream).astype(jnp.float32) + jnp.dot(
            reorder(every_latent), embed_weight, preferred_element_type=jnp.float32
        )
        own, _ = halves(modulate(every_hidden))
        side_rows = tensor_rows(from_side, n_tensor)
        pair_rows = tensor_rows(from_pair, n_tensor)

        def first_product(rows, found):
            preact = None
            for k in range(line):
                term = jnp.dot(rows[k], found[k], preferred_element_type=jnp.float32)
                preact = term if preact is None else preact + term
            return preact

        here = [jnp.concatenate([own[k], side_rows[k]], axis=0) for k in range(line)]
        early = first_product(here, ups[0])
        from_both, early = lax.optimization_barrier((from_both, early))
        both_rows = tensor_rows(from_both, n_tensor)
        there = [
            jnp.concatenate([pair_rows[k ^ 1], both_rows[k ^ 1]], axis=0) for k in range(line)
        ]

        acts, gates = [], []
        top = tokens // 2
        for rows in (here, there):
            kept, given = [], []
            for found in ups:
                if rows is here and found is ups[0]:
                    preact = early
                else:
                    preact = first_product(rows, found)
                came = lax.ppermute(preact[tokens:].astype(jnp.bfloat16), "tm", swap)
                activated = jax.nn.gelu(
                    preact[:tokens] + came.astype(jnp.float32), approximate=True
                ).astype(jnp.bfloat16)
                across = lax.ppermute(activated, "tm", swap)
                kept.append(jnp.concatenate([activated[:top], across[:top]], axis=0))
                given.append(jnp.concatenate([activated[top:], across[top:]], axis=0))
            gates.append(activated)
            acts.append((jnp.concatenate(kept, axis=1), jnp.concatenate(given, axis=1)))

        near, far = [], []
        bunch = max(line // 2, 2)
        for start in range(0, line, bunch):
            count = bunch
            gate = gates[min(start // bunch, 1)]
            arrived, _ = lax.optimization_barrier((downs[start : start + bunch], gate))
            block = jnp.concatenate(arrived, axis=1)
            sums = []
            for act_kept, act_given in acts:
                given = jnp.dot(act_given, block, preferred_element_type=jnp.float32)
                kept = jnp.dot(act_kept, block, preferred_element_type=jnp.float32)
                given = given.astype(jnp.bfloat16).reshape(2, top, -1)
                kept = kept.astype(jnp.bfloat16).reshape(2, top, -1)
                sums.append(tensor_sum(kept, given, n_tensor))
            back = lax.ppermute(sums[1].astype(jnp.bfloat16), "tm", pair).astype(jnp.float32)
            back = jnp.concatenate(
                [back[:, :, (j ^ 1) * depth : ((j ^ 1) + 1) * depth] for j in range(count)], axis=-1
            )
            total = sums[0] + back
            crossed = lax.ppermute(total[1].astype(jnp.bfloat16), "tm", swap).astype(jnp.float32)
            for j in range(count):
                near.append(total[0][:, j * depth : (j + 1) * depth])
                far.append(crossed[:, j * depth : (j + 1) * depth])
        near, far = by_slot(near, place), by_slot(far, place)
        pieces = []
        for a, b in zip(near, far):
            pieces.append(jnp.where(side == 0, a, b))
            pieces.append(jnp.where(side == 0, b, a))
        mixed = jnp.concatenate(pieces, axis=-1)

        updated = hidden + modulation[2] * mixed
        drift = jnp.dot(
            normalize(updated).astype(jnp.bfloat16), head_weight, preferred_element_type=jnp.float32
        )
        first = (position == 0).astype(jnp.float32)
        term = first * latent - step_sizes[0] * drift
        beside = lax.ppermute(term, "tm", swap)
        couple = term + beside
        new_latent = term + jnp.where(side == 1, beside, 0.0)
        for k in range(1, line):
            ahead = [(i, i + 2 * k) for i in range(n_tm - 2 * k)]
            new_latent = new_latent + lax.ppermute(couple, "tm", ahead)
        return (drift[None], new_latent[None])

    return local


def solution(mesh):
    in_specs = (
        P("tm", "tensor", None),
        P("tm", None, None),
        P("tm"),
        P("tm"),
        P(),
        P(None, None, "tensor"),
        P("tm", "tensor"),
        P("tensor", "tm"),
        P(),
    )
    out_specs = (P("tm", "tensor", None), P("tm", "tensor", None))
    local = make_local(mesh.shape["tm"], mesh.shape["tensor"])
    return jax.shard_map(local, mesh=mesh, in_specs=in_specs, out_specs=out_specs, check_vma=False)
```

```python
import math

import jax
import jax.numpy as jnp
from jax import lax
from jax.sharding import PartitionSpec as P


def normalize(values):
    centre = values - jnp.mean(values, axis=-1, keepdims=True)
    spread = jnp.mean(centre * centre, axis=-1, keepdims=True)
    return centre * lax.rsqrt(spread + 1e-06)


def time_features(stamps, width):
    half = width // 2
    freqs = jnp.exp(-math.log(10000.0) * jnp.arange(half, dtype=jnp.float32) / half)
    angles = stamps.astype(jnp.float32)[:, None] * freqs[None, :]
    return jnp.concatenate([jnp.cos(angles), jnp.sin(angles)], axis=-1)


def row_order(count):
    order, shift = [0], count // 2
    while shift >= 1:
        order = order + [j ^ shift for j in order]
        shift //= 2
    return order


def tensor_sum(kept, given, count):
    shift = 1
    while shift < count:
        got = lax.ppermute(
            given.astype(jnp.bfloat16), "tensor", [(t, t ^ shift) for t in range(count)]
        )
        kept = kept.astype(jnp.float32) + got.astype(jnp.float32)
        rows = kept.shape[1] // 2
        shift *= 2
        if shift < count:
            kept, given = kept[:, :rows], kept[:, rows:]
    return kept


def by_slot(blocks, place):
    bit = 1
    while bit < len(blocks):
        take = (place // bit) % 2 == 1
        blocks = [jnp.where(take, blocks[k ^ bit], blocks[k]) for k in range(len(blocks))]
        bit *= 2
    return blocks


def tensor_rows(part, count):
    shift = count // 2
    while shift >= 1:
        got = lax.ppermute(part, "tensor", [(t, t ^ shift) for t in range(count)])
        part = jnp.concatenate([part, got], axis=1)
        shift //= 2
    return part


def make_local(n_tm, n_tensor):
    line = n_tm // 2
    swap = [(i, i ^ 1) for i in range(n_tm)]
    pair = [(i, i ^ 2) for i in range(n_tm)]

    def reach(values, k):
        return lax.ppermute(values, "tm", [(i, i ^ (2 * k)) for i in range(n_tm)])

    def local(
        latents,
        residual,
        timesteps,
        step_sizes,
        embed_weight,
        mod_weight,
        up_weight,
        down_weight,
        head_weight,
    ):
        position = lax.axis_index("tm")
        column = lax.axis_index("tensor")
        place, side = position // 2, position % 2
        even = place % 2 == 0
        latent = latents[0]
        stream = residual[0]
        tokens, width = stream.shape
        own_rows = latent.shape[0]
        depth = up_weight.shape[0]
        half = up_weight.shape[1] // 2
        first_cut = -(-half // 256) * 128
        cuts = [(0, first_cut), (first_cut, half)]

        ups = []
        before = None
        for a, b in cuts:
            low, high = up_weight[:, a:b], up_weight[:, half + a : half + b]
            kept, given = jnp.where(even, low, high), jnp.where(even, high, low)
            found = [kept]
            for k in range(1, line):
                block = given if k % 2 else kept
                if before is not None:
                    block, _ = lax.optimization_barrier((block, before[k]))
                found.append(reach(block, k))
            ups.append(found)
            before = found
        parity = place % 2
        down_kept = lax.dynamic_slice_in_dim(down_weight, parity * half, half, 0)
        down_given = lax.dynamic_slice_in_dim(down_weight, (1 - parity) * half, half, 0)

        feature = jax.nn.silu(time_features(timesteps, mod_weight.shape[1])).astype(jnp.bfloat16)[0]
        piece_mod = jnp.einsum("f,kfd->kd", feature, mod_weight, preferred_element_type=jnp.float32)
        modulation = lax.all_gather(piece_mod, "tensor", axis=1, tiled=True)
        latent_bf = latent.astype(jnp.bfloat16)
        every_latent = lax.all_gather(latent_bf, "tensor", axis=0, tiled=True)

        def modulate(values):
            return (normalize(values) * (1.0 + modulation[1]) + modulation[0]).astype(jnp.bfloat16)

        def halves(values):
            blocks = [values[:, k * depth : (k + 1) * depth] for k in range(2 * line)]
            mine = [jnp.where(side == 0, blocks[2 * k], blocks[2 * k + 1]) for k in range(line)]
            other = [jnp.where(side == 0, blocks[2 * k + 1], blocks[2 * k]) for k in range(line)]
            return by_slot(mine, place), by_slot(other, place)

        row_start = column * own_rows
        hidden = lax.dynamic_slice_in_dim(stream, row_start, own_rows, 0).astype(
            jnp.float32
        ) + jnp.dot(latent_bf, embed_weight, preferred_element_type=jnp.float32)
        mine, other = halves(modulate(hidden))
        from_side = lax.ppermute(jnp.stack(other), "tm", swap)
        from_pair = lax.ppermute(jnp.stack(mine), "tm", pair)
        from_both = lax.ppermute(from_side, "tm", pair)
        order = row_order(n_tensor)

        def reorder(values):
            blocks = [values[t * own_rows : (t + 1) * own_rows] for t in range(n_tensor)]
            blocks = by_slot(blocks, column)
            return jnp.concatenate([blocks[j] for j in order], axis=0)

        every_hidden = reorder(stream).astype(jnp.float32) + jnp.dot(
            reorder(every_latent), embed_weight, preferred_element_type=jnp.float32
        )
        own, _ = halves(modulate(every_hidden))
        side_rows = tensor_rows(from_side, n_tensor)
        pair_rows = tensor_rows(from_pair, n_tensor)

        def first_product(rows, found):
            preact = None
            for k in range(line):
                term = jnp.dot(rows[k], found[k], preferred_element_type=jnp.float32)
                preact = term if preact is None else preact + term
            return preact

        here = [jnp.concatenate([own[k], side_rows[k]], axis=0) for k in range(line)]
        early = first_product(here, ups[0])
        from_both, _ = lax.optimization_barrier((from_both, early))
        downs = [down_kept]
        for k in range(1, line):
            block = down_given if k % 2 else down_kept
            block, _, _ = lax.optimization_barrier((block, before[k], early))
            downs.append(reach(block, k))
        both_rows = tensor_rows(from_both, n_tensor)
        there = [
            jnp.concatenate([pair_rows[k ^ 1], both_rows[k ^ 1]], axis=0) for k in range(line)
        ]

        acts, gates = [], []
        top = tokens // 2
        for rows in (here, there):
            kept, given = [], []
            for found in ups:
                if rows is here and found is ups[0]:
                    preact = early
                else:
                    preact = first_product(rows, found)
                came = lax.ppermute(preact[tokens:].astype(jnp.bfloat16), "tm", swap)
                activated = jax.nn.gelu(
                    preact[:tokens] + came.astype(jnp.float32), approximate=True
                ).astype(jnp.bfloat16)
                across = lax.ppermute(activated, "tm", swap)
                kept.append(jnp.concatenate([activated[:top], across[:top]], axis=0))
                given.append(jnp.concatenate([activated[top:], across[top:]], axis=0))
            gates.append(preact)
            acts.append((jnp.concatenate(kept, axis=1), jnp.concatenate(given, axis=1)))

        near, far = [], []
        bunch = max(line // 2, 2)
        for start in range(0, line, bunch):
            count = bunch
            gate = gates[1] if start == 0 else acts[1][0]
            arrived, _ = lax.optimization_barrier((downs[start : start + bunch], gate))
            block = jnp.concatenate(arrived, axis=1)
            sums = []
            for act_kept, act_given in acts:
                given = jnp.dot(act_given, block, preferred_element_type=jnp.float32)
                kept = jnp.dot(act_kept, block, preferred_element_type=jnp.float32)
                given = given.astype(jnp.bfloat16).reshape(2, top, -1)
                kept = kept.astype(jnp.bfloat16).reshape(2, top, -1)
                sums.append(tensor_sum(kept, given, n_tensor))
            back = lax.ppermute(sums[1].astype(jnp.bfloat16), "tm", pair).astype(jnp.float32)
            back = jnp.concatenate(
                [back[:, :, (j ^ 1) * depth : ((j ^ 1) + 1) * depth] for j in range(count)], axis=-1
            )
            total = sums[0] + back
            crossed = lax.ppermute(total[1].astype(jnp.bfloat16), "tm", swap).astype(jnp.float32)
            for j in range(count):
                near.append(total[0][:, j * depth : (j + 1) * depth])
                far.append(crossed[:, j * depth : (j + 1) * depth])
        near, far = by_slot(near, place), by_slot(far, place)
        pieces = []
        for a, b in zip(near, far):
            pieces.append(jnp.where(side == 0, a, b))
            pieces.append(jnp.where(side == 0, b, a))
        mixed = jnp.concatenate(pieces, axis=-1)

        updated = hidden + modulation[2] * mixed
        drift = jnp.dot(
            normalize(updated).astype(jnp.bfloat16), head_weight, preferred_element_type=jnp.float32
        )
        first = (position == 0).astype(jnp.float32)
        term = first * latent - step_sizes[0] * drift
        beside = lax.ppermute(term, "tm", swap)
        couple = term + beside
        new_latent = term + jnp.where(side == 1, beside, 0.0)
        for k in range(1, line):
            ahead = [(i, i + 2 * k) for i in range(n_tm - 2 * k)]
            new_latent = new_latent + lax.ppermute(couple, "tm", ahead)
        return (drift[None], new_latent[None])

    return local


def solution(mesh):
    in_specs = (
        P("tm", "tensor", None),
        P("tm", None, None),
        P("tm"),
        P("tm"),
        P(),
        P(None, None, "tensor"),
        P("tm", "tensor"),
        P("tensor", "tm"),
        P(),
    )
    out_specs = (P("tm", "tensor", None), P("tm", "tensor", None))
    local = make_local(mesh.shape["tm"], mesh.shape["tensor"])
    return jax.shard_map(local, mesh=mesh, in_specs=in_specs, out_specs=out_specs, check_vma=False)
```
